32 devices in a mesh: pw: 4 (over z), band: 8 (over y, x, core).
Axes of the slice: x: 2, y: 2, z: 4, core: 2. Of those that a mesh axis runs over, the one named last changes fastest.
Arguments:
- strength: bfloat16 [16128, 16128], P('pw', 'band'), may hold values from -0.046875 to 0.046875
- frequency: bfloat16 [16128, 16128], P('pw', 'band'), may hold values from 0.5 to 2
- left_elements: bfloat16 [16, 128, 16128], P(None, 'band', 'pw'), may hold values from -0.01171875 to 0.01171875
- right_elements: bfloat16 [16, 128, 16128], P(None, None, 'band'), may hold values from -6 to 6
- band_energy: float32 [16], replicated, may hold values from -1.5 to 1.5
- energies: float32 [2], replicated, may hold values from -1 to 1
- occupied: int32 [16], replicated, may hold values 0 or 1
Outputs:
- sigma: float32 [2, 128, 128], P(None, 'band')
The draws below stay inside these ranges and needn't reach their ends.
Inputs may be any that keep to these rules, and one draw needn't show every extreme that they name: 1 marks an occupied band, 0 an empty one.
All inputs are finite; a program needn't handle non-finite values.
Results may differ from the reference program's by a relative error of at most 0.004.
Values may be sent and summed in bfloat16 or wider, within the bound.
No kernel may reach another device: no remote copies, remote signals or barrier semaphores. Data moves between devices by JAX's collectives and lax.ppermute only.
A program may use at most 448 MiB of HBM per device.

```python
import math
import jax
import jax.numpy as jnp
from jax import lax

NG = 16128
NB = 16
NT = 128
NE = 2
N_BAND = 8


def touch_ends(array, stream_key, smallest, top_value):
    index_at = [jax.random.randint(jax.random.fold_in(stream_key, axis), (), 0, length) for axis, length in enumerate(array.shape)]
    widest = array.shape.index(max(array.shape))
    beside = index_at[:widest] + [(index_at[widest] + 1) % array.shape[widest]] + index_at[widest + 1:]
    return array.at[tuple(index_at)].set(smallest).at[tuple(beside)].set(top_value)


def steps_of(stream_key, extent, cuts, smallest, top_value):
    level = 1.0
    for axis_at, parts in cuts:
        heights = jax.random.uniform(jax.random.fold_in(jax.random.fold_in(stream_key, 6), axis_at), (parts,), jnp.float32, smallest / len(cuts), top_value / len(cuts))
        level = level * jnp.repeat(jnp.exp(heights), extent[axis_at] // parts).reshape((-1,) + (1,) * (len(extent) - 1 - axis_at))
    return level


def noise(key, dims, width, reach, cuts=(), held_as=jnp.bfloat16):
    loudness = steps_of(key, dims, cuts, -0.22, 0.18) if cuts else 1.0
    entries = jax.random.normal(key, dims, jnp.float32) * width * loudness
    return jnp.minimum(jnp.maximum(entries, -reach), reach).astype(held_as)


def setup_inputs(seed: int = 0) -> dict:
    arg_keys = jax.random.split(jax.random.key(seed), 8)
    strength = noise(arg_keys[0], (NG, NG), NG ** -0.5, 0.046875, ((0, 4), (1, 8)))
    frequency = jnp.clip(jnp.exp(math.log(2.0) - 1.3862944 * jax.random.uniform(arg_keys[1], (NG, NG), jnp.float32) ** steps_of(arg_keys[1], (NG, NG), ((0, 4), (1, 8)), -0.2, 0.2)), 0.5, 2.0).astype(jnp.bfloat16)
    left_elements = noise(arg_keys[2], (NB, NT, NG), (NG * NB) ** -0.5, 0.01171875, ((1, 8), (2, 4)))
    right_elements = noise(arg_keys[3], (NB, NT, NG), 1.0, 6.0, ((2, 8),))
    band_energy = jnp.clip(jax.random.uniform(arg_keys[4], (NB,), jnp.float32, -1.5, 1.5), -1.5, 1.5)
    energies = jnp.clip(jax.random.uniform(arg_keys[5], (NE,), jnp.float32, -1.0, 1.0), -1.0, 1.0)
    occupied = touch_ends((jax.random.randint(arg_keys[6], (NB,), 0, 2) < 1).astype(jnp.int32), jax.random.fold_in(arg_keys[6], 1), 0, 1)
    return dict(strength=strength, frequency=frequency, left_elements=left_elements, right_elements=right_elements, band_energy=band_energy, energies=energies, occupied=occupied)


def reference(strength, frequency, left_elements, right_elements, band_energy, energies, occupied):
    sign_band = 1.0 - 2.0 * occupied.astype(jnp.float32)
    columns = NG // N_BAND

    def per_band(total, band_index):
        left_rows = left_elements[band_index].astype(jnp.float32)
        right_rows = right_elements[band_index]
        offsets = energies - band_energy[band_index]

        def per_block(inner, column_block):
            first = (column_block * columns).astype(jnp.int32)
            strength_block = lax.dynamic_slice_in_dim(strength, first, columns, 1).astype(jnp.float32)
            frequency_block = lax.dynamic_slice_in_dim(frequency, first, columns, 1).astype(jnp.float32)
            shift = offsets[:, None, None] - sign_band[band_index] * frequency_block[None]
            factor = strength_block[None] * shift / (frequency_block[None] * (shift * shift + 0.01))
            factor = factor.astype(jnp.bfloat16).astype(jnp.float32)
            right_block = lax.dynamic_slice_in_dim(right_rows, first, columns, 1).astype(jnp.float32)
            weighted = jnp.einsum('egh,mh->egm', factor, right_block)
            weighted = weighted.astype(jnp.bfloat16).astype(jnp.float32)
            contribution = jnp.einsum('ng,egm->enm', left_rows, weighted)
            return inner + contribution, None

        total, _ = lax.scan(per_block, total, jnp.arange(N_BAND, dtype=jnp.int32))
        return total, None

    start = jnp.zeros((NE, NT, NT), jnp.float32)
    sigma, _ = lax.scan(per_band, start, jnp.arange(NB, dtype=jnp.int32))
    return sigma
```

```python
import math

import jax
import jax.numpy as jnp
from jax import lax
from jax.experimental import pallas as pl
from jax.experimental.pallas import tpu as pltpu
from jax.sharding import PartitionSpec as P


WIDTH = 0.01
CHUNK = 256
ROWS = 224
f32, bf16 = jnp.float32, jnp.bfloat16


def rows_of(count):
    return max(r for r in range(16, ROWS + 1, 16) if count % r == 0)


def weighted_call(strength, frequency, right, band_energy, energies, occupied):
    row_count, column_count = strength.shape
    band_count, target_count, _ = right.shape
    rows = rows_of(row_count)
    steps = row_count // rows
    chunks = -(-column_count // CHUNK)
    tail = column_count - (chunks - 1) * CHUNK
    tail_at = column_count - tail
    loops = band_count // 2
    in_loop = min(chunks - 1, loops)
    unit = 1.0 / math.sqrt(2.0 * WIDTH)

    def kernel(be, en, oc, freq0, str0, freq, stren, right_ref, out, ws, ts, fa, fb, right_tail):
        g = pl.program_id(0)
        cur = g % 2
        nxt = 1 - cur
        e0 = en[0] * unit
        e1 = en[1] * unit
        half = 0.5 * (e1 - e0)
        k1 = 0.5 - half * half
        k2 = 2.0 * half * half

        def convert(w, s):
            w = w.astype(f32)
            return w * unit, (s.astype(f32) / w) * unit

        def convert_chunk(w_ref, s_ref, slot, c):
            lanes = slice(c * CHUNK, (c + 1) * CHUNK)
            ws[slot, c], ts[slot, c] = convert(w_ref[:, lanes], s_ref[:, lanes])

        def convert_tail(w_ref, s_ref, slot):
            w, s = convert(w_ref[:, tail_at:column_count], s_ref[:, tail_at:column_count])
            ws[slot, chunks - 1, :, 0:tail] = w
            ts[slot, chunks - 1, :, 0:tail] = s

        def center_of(b):
            sign = (1 - 2 * oc[b]).astype(f32)
            return sign * (0.5 * (e0 + e1) - be[b] * unit)

        def factors(slot, c, center, dst):
            for lo in range(0, rows, 16):
                mu = ws[slot, c, lo : lo + 16] - center
                t = mu * mu + k1
                r = ts[slot, c, lo : lo + 16] / (t * t + k2)
                x = r * t
                dst[c, lo : lo + 16, :] = (mu * x).astype(bf16)
                dst[c, rows + lo : rows + lo + 16, :] = (r - x).astype(bf16)

        def step(slot, b_next, dst, b, src):
            center = center_of(b_next)
            total = None
            for c in range(chunks):
                factors(slot, c, center, dst)
                lanes = slice(c * CHUNK, (c + 1) * CHUNK)
                rhs = right_tail[b] if c == chunks - 1 else right_ref[b, :, lanes]
                part = lax.dot_general(
                    src[c], rhs, (((1,), (1,)), ((), ())), preferred_element_type=f32
                )
                total = part if total is None else total + part
            sign = (2 * oc[b] - 1).astype(f32)
            even = total[:rows] * sign
            odd = total[rows:] * half
            out[b, :, 0:target_count] = (even - odd).astype(bf16)
            out[b, :, target_count:] = (even + odd).astype(bf16)

        @pl.when(g == 0)
        def _():
            for b in range(band_count):
                right_tail[b] = jnp.zeros((target_count, CHUNK), bf16)
                right_tail[b, :, 0:tail] = right_ref[b, :, tail_at:column_count]
            for slot in range(2):
                ws[slot, chunks - 1] = jnp.ones((rows, CHUNK), f32)
                ts[slot, chunks - 1] = jnp.zeros((rows, CHUNK), f32)
            for c in range(chunks - 1):
                convert_chunk(freq0, str0, 0, c)
            convert_tail(freq0, str0, 0)
            for c in range(chunks):
                factors(0, c, center_of(0), fa)

        for c in range(in_loop, chunks - 1):
            convert_chunk(freq, stren, nxt, c)
        convert_tail(freq, stren, nxt)

        def pair(i, _):
            if in_loop:
                c = jnp.minimum(i, in_loop - 1)
                lanes = pl.ds(pl.multiple_of(c * CHUNK, CHUNK), CHUNK)
                ws[nxt, c], ts[nxt, c] = convert(freq[:, lanes], stren[:, lanes])
            step(cur, 2 * i + 1, fb, 2 * i, fa)
            last = i == loops - 1
            step(jnp.where(last, nxt, cur), jnp.where(last, 0, 2 * i + 2), fa, 2 * i + 1, fb)
            return 0

        lax.fori_loop(0, loops, pair, 0)

    scalars = pl.BlockSpec(memory_space=pltpu.SMEM)
    first = pl.BlockSpec((rows, column_count), lambda g: (0, 0), pipeline_mode=pl.Buffered(1))
    ahead = pl.BlockSpec((rows, column_count), lambda g: (jnp.minimum(g + 1, steps - 1), 0))
    return pl.pallas_call(
        kernel,
        name="weighted",
        grid=(steps,),
        in_specs=[
            scalars,
            scalars,
            scalars,
            first,
            first,
            ahead,
            ahead,
            pl.BlockSpec(right.shape, lambda g: (0, 0, 0), pipeline_mode=pl.Buffered(1)),
        ],
        out_specs=pl.BlockSpec((band_count, rows, 2 * target_count), lambda g: (0, g, 0)),
        out_shape=jax.ShapeDtypeStruct((band_count, row_count, 2 * target_count), bf16),
        scratch_shapes=[
            pltpu.VMEM((2, chunks, rows, CHUNK), f32),
            pltpu.VMEM((2, chunks, rows, CHUNK), f32),
            pltpu.VMEM((chunks, 2 * rows, CHUNK), bf16),
            pltpu.VMEM((chunks, 2 * rows, CHUNK), bf16),
            pltpu.VMEM((band_count, target_count, CHUNK), bf16),
        ],
        compiler_params=pltpu.CompilerParams(
            vmem_limit_bytes=60 << 20
        ),
    )(band_energy, energies, occupied, frequency, strength, frequency, strength, right)


def sum_over(x, axis, size):
    if size > 8:
        return lax.psum(x, axis)
    total = x
    for d in range(1, size):
        total = total + lax.ppermute(x, axis, [(i, (i + d) % size) for i in range(size)])
    return total


def solution(mesh):
    band_size = mesh.shape["band"]
    pw_size = mesh.shape["pw"]

    def body(strength, frequency, left, right, band_energy, energies, occupied):
        target_count = right.shape[1]
        left_all = lax.all_gather(left, "band", axis=1, tiled=True)
        weighted = weighted_call(strength, frequency, right, band_energy, energies, occupied)
        partial = jnp.einsum("bng,bgx->nx", left_all, weighted, preferred_element_type=f32)
        pieces = partial.reshape(band_size, target_count // band_size, -1)
        pieces = lax.all_to_all(pieces, "band", split_axis=0, concat_axis=0, tiled=True)
        total = sum_over(pieces.sum(0), "pw", pw_size)
        return total.reshape(-1, 2, target_count).transpose(1, 0, 2)

    return jax.shard_map(
        body,
        mesh=mesh,
        in_specs=(
            P("pw", "band"),
            P("pw", "band"),
            P(None, "band", "pw"),
            P(None, None, "band"),
            P(),
            P(),
            P(),
        ),
        out_specs=P(None, "band", None),
        check_vma=False,
    )
```

```python
import math

import jax
import jax.numpy as jnp
from jax import lax
from jax.experimental import pallas as pl
from jax.experimental.pallas import tpu as pltpu
from jax.sharding import PartitionSpec as P


WIDTH = 0.01
CHUNK = 256
ROWS = 224
f32, bf16 = jnp.float32, jnp.bfloat16


def rows_of(count):
    return max(r for r in range(16, ROWS + 1, 16) if count % r == 0)


def first_bands(band_count):
    return (band_count * 3 // 8) // 2 * 2


def band_call(strength, frequency, right, scalars, first, last, left=None, earlier=None):
    row_count, column_count = strength.shape
    target_count = right.shape[2]
    bands = last - first
    rows = rows_of(row_count)
    steps = row_count // rows
    chunks = -(-column_count // CHUNK)
    tail = column_count - (chunks - 1) * CHUNK
    tail_at = column_count - tail
    loops = bands // 2
    per_loop = -(-(chunks - 1) // loops)
    unit = 1.0 / math.sqrt(2.0 * WIDTH)
    fused = left is not None

    def kernel(*refs):
        be, en, oc, freq0, str0, freq, stren, right_hbm = refs[:8]
        if fused:
            left_ref, early, out, ws, ts, fa, fb, rt, sem, wa, wb = refs[8:]
        else:
            out, ws, ts, fa, fb, rt, sem = refs[8:]
        g = pl.program_id(0)
        cur = g % 2
        nxt = 1 - cur
        e0 = en[0] * unit
        e1 = en[1] * unit
        half = 0.5 * (e1 - e0)
        k1 = 0.5 - half * half
        k2 = 2.0 * half * half

        def convert(w, s):
            w = w.astype(f32)
            return w * unit, s.astype(f32) / w

        def convert_at(w_ref, s_ref, slot, c):
            lanes = pl.ds(pl.multiple_of(c * CHUNK, CHUNK), CHUNK)
            ws[slot, c], ts[slot, c] = convert(w_ref[:, lanes], s_ref[:, lanes])

        def convert_tail(w_ref, s_ref, slot):
            w, s = convert(w_ref[:, tail_at:column_count], s_ref[:, tail_at:column_count])
            ws[slot, chunks - 1, :, 0:tail] = w
            ts[slot, chunks - 1, :, 0:tail] = s

        def center_of(b):
            sign = (1 - 2 * oc[first + b]).astype(f32)
            return sign * (0.5 * (e0 + e1) - be[first + b] * unit)

        def factors(slot, c, center, dst):
            for lo in range(0, rows, 16):
                mu = ws[slot, c, lo : lo + 16] - center
                t = mu * mu + k1
                r = ts[slot, c, lo : lo + 16] / (t * t + k2)
                x = r * t
                dst[c, lo : lo + 16, :] = (mu * x).astype(bf16)
                dst[c, rows + lo : rows + lo + 16, :] = (r - x).astype(bf16)

        def add_left(b, w):
            out[...] += jnp.dot(left_ref[b], w, preferred_element_type=f32)

        def step(slot, b_next, dst, b, src, w_prev, w_this):
            center = center_of(b_next)
            total = None
            for c in range(chunks):
                factors(slot, c, center, dst)
                rhs = rt[b, c * CHUNK : (c + 1) * CHUNK, :]
                part = jnp.dot(src[c], rhs, preferred_element_type=f32)
                total = part if total is None else total + part
            if fused:
                add_left(jnp.maximum(first + b - 1, 0), w_prev[...])
            w_this[:, 0:target_count] = (total[:rows] * (2 * oc[first + b] - 1).astype(f32)).astype(bf16)
            w_this[:, target_count:] = total[rows:].astype(bf16)

        @pl.when(g == 0)
        def _():
            copy = pltpu.make_async_copy(
                right_hbm.at[pl.ds(first, bands)], rt.at[:, pl.ds(0, column_count), :], sem
            )
            copy.start()
            if column_count < chunks * CHUNK:
                for b in range(bands):
                    rt[b, column_count:, :] = jnp.zeros((chunks * CHUNK - column_count, target_count), bf16)
            for slot in range(2):
                ws[slot, chunks - 1] = jnp.ones((rows, CHUNK), f32)
                ts[slot, chunks - 1] = jnp.zeros((rows, CHUNK), f32)
            if fused:
                out[...] = jnp.zeros_like(out)
                wb[...] = jnp.zeros_like(wb)
            convert_tail(freq0, str0, 0)
            if chunks > 1:

                def one(c, _):
                    convert_at(freq0, str0, 0, c)
                    return 0

                lax.fori_loop(0, chunks - 1, one, 0)

            def fill(c, _):
                factors(0, c, center_of(0), fa)
                return 0

            lax.fori_loop(0, chunks, fill, 0)
            copy.wait()

        convert_tail(freq, stren, nxt)
        if fused:
            for b in range(loops, first):
                add_left(b, early[b])

        def pair(i, _):
            for k in range(per_loop):
                convert_at(freq, stren, nxt, jnp.minimum(i * per_loop + k, chunks - 2))
            if fused:
                add_left(i, early[i])
            wa_, wb_ = (wa, wb) if fused else (out.at[2 * i], out.at[2 * i + 1])
            step(cur, 2 * i + 1, fb, 2 * i, fa, wb_, wa_)
            end = i == loops - 1
            step(jnp.where(end, nxt, cur), jnp.where(end, 0, 2 * i + 2), fa, 2 * i + 1, fb, wa_, wb_)
            return 0

        lax.fori_loop(0, loops, pair, 0)
        if fused:
            add_left(last - 1, wb[...])
            wb[...] = jnp.zeros_like(wb)

    smem = pl.BlockSpec(memory_space=pltpu.SMEM)
    start = pl.BlockSpec((rows, column_count), lambda g: (0, 0), pipeline_mode=pl.Buffered(1))
    ahead = pl.BlockSpec((rows, column_count), lambda g: (jnp.minimum(g + 1, steps - 1), 0))
    in_specs = [smem, smem, smem, start, start, ahead, ahead, pl.BlockSpec(memory_space=pl.ANY)]
    operands = [*scalars, frequency, strength, frequency, strength, right]
    scratch = [
        pltpu.VMEM((2, chunks, rows, CHUNK), f32),
        pltpu.VMEM((2, chunks, rows, CHUNK), f32),
        pltpu.VMEM((chunks, 2 * rows, CHUNK), bf16),
        pltpu.VMEM((chunks, 2 * rows, CHUNK), bf16),
        pltpu.VMEM((bands, chunks * CHUNK, target_count), bf16),
        pltpu.SemaphoreType.DMA,
    ]
    wide = 2 * target_count
    if fused:
        in_specs += [
            pl.BlockSpec((left.shape[0], None, target_count, rows), lambda g: (0, g, 0, 0)),
            pl.BlockSpec((first, rows, wide), lambda g: (0, g, 0)),
        ]
        operands += [left, earlier]
        out_specs = pl.BlockSpec((target_count, wide), lambda g: (0, 0))
        out_shape = jax.ShapeDtypeStruct((target_count, wide), f32)
        scratch += [pltpu.VMEM((rows, wide), bf16), pltpu.VMEM((rows, wide), bf16)]
    else:
        out_specs = pl.BlockSpec((bands, rows, wide), lambda g: (0, g, 0))
        out_shape = jax.ShapeDtypeStruct((bands, row_count, wide), bf16)
    return pl.pallas_call(
        kernel,
        name="summed" if fused else "weighted",
        grid=(steps,),
        in_specs=in_specs,
        out_specs=out_specs,
        out_shape=out_shape,
        scratch_shapes=scratch,
        compiler_params=pltpu.CompilerParams(
            vmem_limit_bytes=60 << 20
        ),
    )(*operands)


def sum_over(x, axis, size):
    if size > 8:
        return lax.psum(x, axis)
    total = x
    for d in range(1, size):
        total = total + lax.ppermute(x, axis, [(i, (i + d) % size) for i in range(size)])
    return total


def solution(mesh):
    band_size = mesh.shape["band"]
    pw_size = mesh.shape["pw"]

    def body(strength, frequency, left, right, band_energy, energies, occupied):
        band_count, target_count, _ = right.shape
        row_count = strength.shape[0]
        rows = rows_of(row_count)
        first = first_bands(band_count)
        scalars = (band_energy, energies, occupied)
        tiles = left.reshape(band_count, -1, row_count // rows, rows).transpose(0, 2, 1, 3)
        left_all = lax.all_gather(tiles, "band", axis=2, tiled=True)
        right_t = right.transpose(0, 2, 1)
        early = band_call(strength, frequency, right_t, scalars, 0, first)
        both = band_call(
            strength, frequency, right_t, scalars, first, band_count, left_all, early
        )
        pieces = both.reshape(band_size, target_count // band_size, -1)
        pieces = lax.all_to_all(pieces, "band", split_axis=0, concat_axis=0, tiled=True)
        total = sum_over(pieces.sum(0), "pw", pw_size)
        even = total[:, :target_count]
        odd = total[:, target_count:] * (0.5 * (energies[1] - energies[0]) / math.sqrt(2.0 * WIDTH))
        return jnp.stack([even - odd, even + odd]) * (1.0 / math.sqrt(2.0 * WIDTH))

    return jax.shard_map(
        body,
        mesh=mesh,
        in_specs=(
            P("pw", "band"),
            P("pw", "band"),
            P(None, "band", "pw"),
            P(None, None, "band"),
            P(),
            P(),
            P(),
        ),
        out_specs=P(None, "band", None),
        check_vma=False,
    )
```

```python
import math

import jax
import jax.numpy as jnp
from jax import lax
from jax.experimental import pallas as pl
from jax.experimental.pallas import tpu as pltpu
from jax.sharding import PartitionSpec as P


WIDTH = 0.01
CHUNK = 256
ROWS = 336
f32, bf16 = jnp.float32, jnp.bfloat16


def rows_of(count):
    return max(r for r in range(16, ROWS + 1, 16) if count % r == 0)


def band_call(strength, frequency, right, scalars, first, last, left=None, earlier=None):
    row_count, column_count = strength.shape
    target_count = right.shape[2]
    bands = last - first
    rows = rows_of(row_count)
    steps = row_count // rows
    chunks = -(-column_count // CHUNK)
    tail = column_count - (chunks - 1) * CHUNK
    tail_at = column_count - tail
    loops = bands // 2
    unit = 1.0 / math.sqrt(2.0 * WIDTH)
    fused = left is not None

    def kernel(*refs):
        be, en, oc, freq0, str0, freq, stren, right_hbm = refs[:8]
        if fused:
            left_ref, early, out, ws, ts, fa, fb, rt, sem, wa, wb = refs[8:]
        else:
            out, ws, ts, fa, fb, rt, sem = refs[8:]
        g = pl.program_id(0)
        cur = g % 2
        nxt = 1 - cur
        e0 = en[0] * unit
        e1 = en[1] * unit
        half = 0.5 * (e1 - e0)
        k1 = 0.5 - half * half
        k2 = 2.0 * half * half

        def convert(w, s):
            w = w.astype(f32)
            return w * unit, s.astype(f32) / w

        def convert_at(w_ref, s_ref, slot, c):
            lanes = pl.ds(pl.multiple_of(c * CHUNK, CHUNK), CHUNK)
            ws[slot, c], ts[slot, c] = convert(w_ref[:, lanes], s_ref[:, lanes])

        def convert_tail(w_ref, s_ref, slot):
            w, s = convert(w_ref[:, tail_at:column_count], s_ref[:, tail_at:column_count])
            ws[slot, chunks - 1, :, 0:tail] = w
            ts[slot, chunks - 1, :, 0:tail] = s

        def center_of(b):
            sign = (1 - 2 * oc[first + b]).astype(f32)
            return sign * (0.5 * (e0 + e1) - be[first + b] * unit)

        def factors(slot, c, center, dst):
            for lo in range(0, rows, 16):
                mu = ws[slot, c, lo : lo + 16] - center
                t = mu * mu + k1
                r = ts[slot, c, lo : lo + 16] / (t * t + k2)
                x = r * t
                dst[c, lo : lo + 16, :] = (mu * x).astype(bf16)
                dst[c, rows + lo : rows + lo + 16, :] = (r - x).astype(bf16)

        def add_left(b, w):
            out[...] += jnp.dot(left_ref[b], w, preferred_element_type=f32)

        def step(slot, b_next, dst, b, src, w_prev, w_this):
            center = center_of(b_next)
            total = None
            for c in range(chunks):
                factors(slot, c, center, dst)
                rhs = rt[b, c * CHUNK : (c + 1) * CHUNK, :]
                part = jnp.dot(src[c], rhs, preferred_element_type=f32)
                total = part if total is None else total + part
            if fused:
                add_left(jnp.maximum(first + b - 1, 0), w_prev[...])
            w_this[:, 0:target_count] = (total[:rows] * (2 * oc[first + b] - 1).astype(f32)).astype(bf16)
            w_this[:, target_count:] = total[rows:].astype(bf16)

        @pl.when(g == 0)
        def _():
            copy = pltpu.make_async_copy(
                right_hbm.at[pl.ds(first, bands)], rt.at[:, pl.ds(0, column_count), :], sem
            )
            copy.start()
            if column_count < chunks * CHUNK:
                for b in range(bands):
                    rt[b, column_count:, :] = jnp.zeros((chunks * CHUNK - column_count, target_count), bf16)
            for slot in range(2):
                ws[slot, chunks - 1] = jnp.ones((rows, CHUNK), f32)
                ts[slot, chunks - 1] = jnp.zeros((rows, CHUNK), f32)
            if fused:
                out[...] = jnp.zeros_like(out)
                wb[...] = jnp.zeros_like(wb)
            convert_tail(freq0, str0, 0)
            if chunks > 1:

                def one(c, _):
                    convert_at(freq0, str0, 0, c)
                    return 0

                lax.fori_loop(0, chunks - 1, one, 0)

            def fill(c, _):
                factors(0, c, center_of(0), fa)
                return 0

            lax.fori_loop(0, chunks, fill, 0)
            copy.wait()

        convert_tail(freq, stren, nxt)
        if chunks > 1:

            def ahead_one(c, _):
                convert_at(freq, stren, nxt, c)
                return 0

            lax.fori_loop(0, chunks - 1, ahead_one, 0)
        if fused:
            for b in range(loops, first):
                add_left(b, early[b])

        def pair(i, _):
            if fused:
                add_left(i, early[i])
            wa_, wb_ = (wa, wb) if fused else (out.at[2 * i], out.at[2 * i + 1])
            step(cur, 2 * i + 1, fb, 2 * i, fa, wb_, wa_)
            end = i == loops - 1
            step(jnp.where(end, nxt, cur), jnp.where(end, 0, 2 * i + 2), fa, 2 * i + 1, fb, wa_, wb_)
            return 0

        lax.fori_loop(0, loops, pair, 0)
        if fused:
            add_left(last - 1, wb[...])
            wb[...] = jnp.zeros_like(wb)

    smem = pl.BlockSpec(memory_space=pltpu.SMEM)
    start = pl.BlockSpec((rows, column_count), lambda g: (0, 0), pipeline_mode=pl.Buffered(1))
    ahead = pl.BlockSpec((rows, column_count), lambda g: (jnp.minimum(g + 1, steps - 1), 0))
    in_specs = [smem, smem, smem, start, start, ahead, ahead, pl.BlockSpec(memory_space=pl.ANY)]
    operands = [*scalars, frequency, strength, frequency, strength, right]
    scratch = [
        pltpu.VMEM((2, chunks, rows, CHUNK), f32),
        pltpu.VMEM((2, chunks, rows, CHUNK), f32),
        pltpu.VMEM((chunks, 2 * rows, CHUNK), bf16),
        pltpu.VMEM((chunks, 2 * rows, CHUNK), bf16),
        pltpu.VMEM((bands, chunks * CHUNK, target_count), bf16),
        pltpu.SemaphoreType.DMA,
    ]
    wide = 2 * target_count
    if fused:
        in_specs += [
            pl.BlockSpec((left.shape[0], None, target_count, rows), lambda g: (0, g, 0, 0)),
            pl.BlockSpec((first, rows, wide), lambda g: (0, g, 0)),
        ]
        operands += [left, earlier]
        out_specs = pl.BlockSpec((target_count, wide), lambda g: (0, 0))
        out_shape = jax.ShapeDtypeStruct((target_count, wide), f32)
        scratch += [pltpu.VMEM((rows, wide), bf16), pltpu.VMEM((rows, wide), bf16)]
    else:
        out_specs = pl.BlockSpec((bands, rows, wide), lambda g: (0, g, 0))
        out_shape = jax.ShapeDtypeStruct((bands, row_count, wide), bf16)
    return pl.pallas_call(
        kernel,
        name="summed" if fused else "weighted",
        grid=(steps,),
        in_specs=in_specs,
        out_specs=out_specs,
        out_shape=out_shape,
        scratch_shapes=scratch,
        compiler_params=pltpu.CompilerParams(
            vmem_limit_bytes=60 << 20
        ),
    )(*operands)


def sum_over(x, axis, size):
    if size > 8:
        return lax.psum(x, axis)
    total = x
    for d in range(1, size):
        total = total + lax.ppermute(x, axis, [(i, (i + d) % size) for i in range(size)])
    return total


def solution(mesh):
    band_size = mesh.shape["band"]
    pw_size = mesh.shape["pw"]

    def body(strength, frequency, left, right, band_energy, energies, occupied):
        band_count, target_count, _ = right.shape
        scalars = (band_energy, energies, occupied)
        left_all = lax.all_gather(left, "band", axis=1, tiled=True)
        weighted = band_call(strength, frequency, right.transpose(0, 2, 1), scalars, 0, band_count)
        both = jnp.einsum("bng,bgx->nx", left_all, weighted, preferred_element_type=f32)
        pieces = both.reshape(band_size, target_count // band_size, -1)
        pieces = lax.all_to_all(pieces, "band", split_axis=0, concat_axis=0, tiled=True)
        total = sum_over(pieces.sum(0), "pw", pw_size)
        even = total[:, :target_count]
        odd = total[:, target_count:] * (0.5 * (energies[1] - energies[0]) / math.sqrt(2.0 * WIDTH))
        return jnp.stack([even - odd, even + odd]) * (1.0 / math.sqrt(2.0 * WIDTH))

    return jax.shard_map(
        body,
        mesh=mesh,
        in_specs=(
            P("pw", "band"),
            P("pw", "band"),
            P(None, "band", "pw"),
            P(None, None, "band"),
            P(),
            P(),
            P(),
        ),
        out_specs=P(None, "band", None),
        check_vma=False,
    )
```

```python
import math

import jax
import jax.numpy as jnp
from jax import lax
from jax.experimental import pallas as pl
from jax.experimental.pallas import tpu as pltpu
from jax.sharding import PartitionSpec as P


WIDTH = 0.01
CHUNK = 256
ROWS = 336
f32, bf16 = jnp.float32, jnp.bfloat16


def rows_of(count):
    return max(r for r in range(16, ROWS + 1, 16) if count % r == 0)


def band_call(strength, frequency, right, scalars):
    row_count, column_count = strength.shape
    bands, _, target_count = right.shape
    rows = rows_of(row_count)
    steps = row_count // rows
    chunks = -(-column_count // CHUNK)
    tail = column_count - (chunks - 1) * CHUNK
    tail_at = column_count - tail
    loops = bands // 2
    unit = 1.0 / math.sqrt(2.0 * WIDTH)

    def kernel(*refs):
        be, en, oc, freq0, str0, freq, stren, right_hbm = refs[:8]
        out, ws, ts, fa, fb, rt, sem = refs[8:]
        g = pl.program_id(0)
        cur = g % 2
        nxt = 1 - cur
        e0 = en[0] * unit
        e1 = en[1] * unit
        half = 0.5 * (e1 - e0)
        k1 = 0.5 - half * half
        k2 = 2.0 * half * half

        def convert(w, s):
            w = w.astype(f32)
            return w * unit, s.astype(f32) / w

        def convert_at(w_ref, s_ref, slot, c):
            lanes = pl.ds(pl.multiple_of(c * CHUNK, CHUNK), CHUNK)
            ws[slot, c], ts[slot, c] = convert(w_ref[:, lanes], s_ref[:, lanes])

        def convert_tail(w_ref, s_ref, slot):
            w, s = convert(w_ref[:, tail_at:column_count], s_ref[:, tail_at:column_count])
            ws[slot, chunks - 1, :, 0:tail] = w
            ts[slot, chunks - 1, :, 0:tail] = s

        def center_of(b):
            sign = (1 - 2 * oc[b]).astype(f32)
            return sign * (0.5 * (e0 + e1) - be[b] * unit)

        def factors(slot, c, center, dst):
            for lo in range(0, rows, 16):
                mu = ws[slot, c, lo : lo + 16] - center
                t = mu * mu + k1
                r = ts[slot, c, lo : lo + 16] / (t * t + k2)
                x = r * t
                dst[c, lo : lo + 16, :] = (mu * x).astype(bf16)
                dst[c, rows + lo : rows + lo + 16, :] = (r - x).astype(bf16)

        def step(slot, b_next, dst, b, src):
            center = center_of(b_next)
            total = None
            for c in range(chunks):
                factors(slot, c, center, dst)
                rhs = rt[b, c * CHUNK : (c + 1) * CHUNK, :]
                part = jnp.dot(src[c], rhs, preferred_element_type=f32)
                total = part if total is None else total + part
            sign = (2 * oc[b] - 1).astype(f32)
            out[b, :, 0:target_count] = (total[:rows] * sign).astype(bf16)
            out[b, :, target_count:] = total[rows:].astype(bf16)

        @pl.when(g == 0)
        def _():
            copy = pltpu.make_async_copy(
                right_hbm, rt.at[:, pl.ds(0, column_count), :], sem
            )
            copy.start()
            if column_count < chunks * CHUNK:
                for b in range(bands):
                    rt[b, column_count:, :] = jnp.zeros((chunks * CHUNK - column_count, target_count), bf16)
            for slot in range(2):
                ws[slot, chunks - 1] = jnp.ones((rows, CHUNK), f32)
                ts[slot, chunks - 1] = jnp.zeros((rows, CHUNK), f32)
            convert_tail(freq0, str0, 0)
            if chunks > 1:

                def one(c, _):
                    convert_at(freq0, str0, 0, c)
                    return 0

                lax.fori_loop(0, chunks - 1, one, 0)

            def fill(c, _):
                factors(0, c, center_of(0), fa)
                return 0

            lax.fori_loop(0, chunks, fill, 0)
            copy.wait()

        convert_tail(freq, stren, nxt)
        if chunks > 1:

            def ahead_one(c, _):
                convert_at(freq, stren, nxt, c)
                return 0

            lax.fori_loop(0, chunks - 1, ahead_one, 0)

        def pair(i, _):
            step(cur, 2 * i + 1, fb, 2 * i, fa)
            end = i == loops - 1
            step(jnp.where(end, nxt, cur), jnp.where(end, 0, 2 * i + 2), fa, 2 * i + 1, fb)
            return 0

        lax.fori_loop(0, loops, pair, 0)

    smem = pl.BlockSpec(memory_space=pltpu.SMEM)
    start = pl.BlockSpec((rows, column_count), lambda g: (0, 0), pipeline_mode=pl.Buffered(1))
    ahead = pl.BlockSpec((rows, column_count), lambda g: (jnp.minimum(g + 1, steps - 1), 0))
    in_specs = [smem, smem, smem, start, start, ahead, ahead, pl.BlockSpec(memory_space=pl.ANY)]
    operands = [*scalars, frequency, strength, frequency, strength, right]
    scratch = [
        pltpu.VMEM((2, chunks, rows, CHUNK), f32),
        pltpu.VMEM((2, chunks, rows, CHUNK), f32),
        pltpu.VMEM((chunks, 2 * rows, CHUNK), bf16),
        pltpu.VMEM((chunks, 2 * rows, CHUNK), bf16),
        pltpu.VMEM((bands, chunks * CHUNK, target_count), bf16),
        pltpu.SemaphoreType.DMA,
    ]
    wide = 2 * target_count
    return pl.pallas_call(
        kernel,
        name="weighted",
        grid=(steps,),
        in_specs=in_specs,
        out_specs=pl.BlockSpec((bands, rows, wide), lambda g: (0, g, 0)),
        out_shape=jax.ShapeDtypeStruct((bands, row_count, wide), bf16),
        scratch_shapes=scratch,
        compiler_params=pltpu.CompilerParams(
            vmem_limit_bytes=60 << 20
        ),
    )(*operands)


def left_call(pieces, weighted, position):
    bands, part, row_count = pieces[0].shape
    wide = weighted.shape[2]
    count = len(pieces)

    def kernel(*refs):
        at, w = refs[0], refs[1]
        parts = refs[2 : 2 + count]
        out, acc = refs[2 + count :]
        b = pl.program_id(0)
        left = jnp.concatenate([p[...] for p in parts], axis=0)
        new = jnp.dot(left, w[...], preferred_element_type=f32)

        @pl.when(b == 0)
        def _():
            acc[...] = new

        @pl.when(b > 0)
        def _():
            acc[...] += new

        @pl.when(b == bands - 1)
        def _():
            for d in range(count):
                row = pl.multiple_of(jnp.bitwise_xor(at[0], d) * part, part)
                out[pl.ds(row, part), :] = acc[d * part : (d + 1) * part, :]

    block = pl.BlockSpec((None, part, row_count), lambda b: (b, 0, 0))
    return pl.pallas_call(
        kernel,
        name="summed",
        grid=(bands,),
        in_specs=[
            pl.BlockSpec(memory_space=pltpu.SMEM),
            pl.BlockSpec((None, row_count, wide), lambda b: (b, 0, 0)),
            *([block] * count),
        ],
        out_specs=pl.BlockSpec((count * part, wide), lambda b: (0, 0)),
        out_shape=jax.ShapeDtypeStruct((count * part, wide), f32),
        scratch_shapes=[pltpu.VMEM((count * part, wide), f32)],
        compiler_params=pltpu.CompilerParams(vmem_limit_bytes=60 << 20),
    )(position, weighted, *pieces)


def swapped(x, axis, size, d):
    return lax.ppermute(x, axis, [(i, i ^ d) for i in range(size)])


def sum_over(x, axis, size):
    if size & (size - 1):
        return lax.psum(x, axis)
    d = 1
    while d < size:
        x = x + swapped(x, axis, size, d)
        d *= 2
    return x


def solution(mesh):
    band_size = mesh.shape["band"]
    pw_size = mesh.shape["pw"]

    def body(strength, frequency, left, right, band_energy, energies, occupied):
        target_count = right.shape[1]
        scalars = (band_energy, energies, occupied)
        direct = band_size in (1, 2, 4, 8) and left.shape[1] % 16 == 0
        if direct:
            pieces = [left] + [swapped(left, "band", band_size, d) for d in range(1, band_size)]
        else:
            left_all = lax.all_gather(left, "band", axis=1, tiled=True)
        weighted = band_call(strength, frequency, right.transpose(0, 2, 1), scalars)
        if direct:
            position = lax.axis_index("band").astype(jnp.int32).reshape(1)
            both = left_call(pieces, weighted, position)
        else:
            both = jnp.einsum("bng,bgx->nx", left_all, weighted, preferred_element_type=f32)
        parts = both.reshape(band_size, target_count // band_size, -1)
        parts = lax.all_to_all(parts, "band", split_axis=0, concat_axis=0, tiled=True)
        total = sum_over(parts.sum(0), "pw", pw_size)
        even = total[:, :target_count]
        odd = total[:, target_count:] * (0.5 * (energies[1] - energies[0]) / math.sqrt(2.0 * WIDTH))
        return jnp.stack([even - odd, even + odd]) * (1.0 / math.sqrt(2.0 * WIDTH))

    return jax.shard_map(
        body,
        mesh=mesh,
        in_specs=(
            P("pw", "band"),
            P("pw", "band"),
            P(None, "band", "pw"),
            P(None, None, "band"),
            P(),
            P(),
            P(),
        ),
        out_specs=P(None, "band", None),
        check_vma=False,
    )
```

```python
import math

import jax
import jax.numpy as jnp
from jax import lax
from jax.experimental import pallas as pl
from jax.experimental.pallas import tpu as pltpu
from jax.sharding import PartitionSpec as P


WIDTH = 0.01
CHUNK = 256
ROWS = 336
f32, bf16 = jnp.float32, jnp.bfloat16


def rows_of(count):
    return max(r for r in range(16, ROWS + 1, 16) if count % r == 0)


def band_call(strength, frequency, right, scalars):
    row_count, column_count = strength.shape
    bands, _, target_count = right.shape
    rows = rows_of(row_count)
    steps = row_count // rows
    chunks = -(-column_count // CHUNK)
    tail = column_count - (chunks - 1) * CHUNK
    tail_at = column_count - tail
    loops = bands // 2
    unit = 1.0 / math.sqrt(2.0 * WIDTH)

    def kernel(*refs):
        be, en, oc, freq0, str0, freq, stren, right_hbm = refs[:8]
        out, ws, ts, fa, fb, rt, sem = refs[8:]
        g = pl.program_id(0)
        cur = g % 2
        nxt = 1 - cur
        e0 = en[0] * unit
        e1 = en[1] * unit
        half = 0.5 * (e1 - e0)
        k1 = 0.5 - half * half
        k2 = 2.0 * half * half

        def convert(w, s):
            w = w.astype(f32)
            return w * unit, s.astype(f32) / w

        def convert_at(w_ref, s_ref, slot, c):
            lanes = pl.ds(pl.multiple_of(c * CHUNK, CHUNK), CHUNK)
            ws[slot, c], ts[slot, c] = convert(w_ref[:, lanes], s_ref[:, lanes])

        def convert_tail(w_ref, s_ref, slot):
            w, s = convert(w_ref[:, tail_at:column_count], s_ref[:, tail_at:column_count])
            ws[slot, chunks - 1, :, 0:tail] = w
            ts[slot, chunks - 1, :, 0:tail] = s

        def center_of(b):
            sign = (1 - 2 * oc[b]).astype(f32)
            return sign * (0.5 * (e0 + e1) - be[b] * unit)

        def factors(slot, c, lo, center, dst):
            mu = ws[slot, c, pl.ds(lo, 16)] - center
            t = mu * mu + k1
            r = ts[slot, c, pl.ds(lo, 16)] / (t * t + k2)
            x = r * t
            dst[c, pl.ds(lo, 16), :] = (mu * x).astype(bf16)
            dst[c, pl.ds(rows + lo, 16), :] = (r - x).astype(bf16)

        def first_factors(dst):
            center = center_of(0)
            piece = max(p for p in (112, 96, 48, 32, 16) if rows % p == 0)

            def one(c, _):
                def part(k, _):
                    for q in range(0, piece, 16):
                        factors(0, c, pl.multiple_of(k * piece + q, 16), center, dst)
                    return 0

                return lax.fori_loop(0, rows // piece, part, 0)

            lax.fori_loop(0, chunks, one, 0)

        def step(slot, b_next, dst, b, src):
            center = center_of(b_next)
            total = None
            for c in range(chunks):
                for lo in range(0, rows, 16):
                    factors(slot, c, lo, center, dst)
                rhs = rt[b, c * CHUNK : (c + 1) * CHUNK, :]
                part = jnp.dot(src[c], rhs, preferred_element_type=f32)
                total = part if total is None else total + part
            sign = (2 * oc[b] - 1).astype(f32)
            out[b, :, 0:target_count] = (total[:rows] * sign).astype(bf16)
            out[b, :, target_count:] = total[rows:].astype(bf16)

        @pl.when(g == 0)
        def _():
            copy = pltpu.make_async_copy(
                right_hbm, rt.at[:, pl.ds(0, column_count), :], sem
            )
            copy.start()
            if column_count < chunks * CHUNK:
                for b in range(bands):
                    rt[b, column_count:, :] = jnp.zeros((chunks * CHUNK - column_count, target_count), bf16)
            for slot in range(2):
                ws[slot, chunks - 1] = jnp.ones((rows, CHUNK), f32)
                ts[slot, chunks - 1] = jnp.zeros((rows, CHUNK), f32)
            convert_tail(freq0, str0, 0)
            if chunks > 1:

                def one(c, _):
                    convert_at(freq0, str0, 0, c)
                    return 0

                lax.fori_loop(0, chunks - 1, one, 0)

            first_factors(fa)
            copy.wait()

        convert_tail(freq, stren, nxt)
        if chunks > 1:

            def ahead_one(c, _):
                convert_at(freq, stren, nxt, c)
                return 0

            lax.fori_loop(0, chunks - 1, ahead_one, 0)

        def pair(i, _):
            step(cur, 2 * i + 1, fb, 2 * i, fa)
            end = i == loops - 1
            step(jnp.where(end, nxt, cur), jnp.where(end, 0, 2 * i + 2), fa, 2 * i + 1, fb)
            return 0

        lax.fori_loop(0, loops, pair, 0)

    smem = pl.BlockSpec(memory_space=pltpu.SMEM)
    start = pl.BlockSpec((rows, column_count), lambda g: (0, 0), pipeline_mode=pl.Buffered(1))
    ahead = pl.BlockSpec((rows, column_count), lambda g: (jnp.minimum(g + 1, steps - 1), 0))
    in_specs = [smem, smem, smem, start, start, ahead, ahead, pl.BlockSpec(memory_space=pl.ANY)]
    operands = [*scalars, frequency, strength, frequency, strength, right]
    scratch = [
        pltpu.VMEM((2, chunks, rows, CHUNK), f32),
        pltpu.VMEM((2, chunks, rows, CHUNK), f32),
        pltpu.VMEM((chunks, 2 * rows, CHUNK), bf16),
        pltpu.VMEM((chunks, 2 * rows, CHUNK), bf16),
        pltpu.VMEM((bands, chunks * CHUNK, target_count), bf16),
        pltpu.SemaphoreType.DMA,
    ]
    wide = 2 * target_count
    return pl.pallas_call(
        kernel,
        name="weighted",
        grid=(steps,),
        in_specs=in_specs,
        out_specs=pl.BlockSpec((bands, rows, wide), lambda g: (0, g, 0)),
        out_shape=jax.ShapeDtypeStruct((bands, row_count, wide), bf16),
        scratch_shapes=scratch,
        compiler_params=pltpu.CompilerParams(
            vmem_limit_bytes=63 << 20
        ),
    )(*operands)


def left_call(pieces, weighted):
    bands, part, row_count = pieces[0].shape
    wide = weighted.shape[2]
    count = len(pieces)

    def kernel(*refs):
        w = refs[0]
        parts = refs[1 : 1 + count]
        out, acc = refs[1 + count :]
        b = pl.program_id(0)
        new = None
        for k in range(2):
            left = jnp.concatenate([p[k] for p in parts], axis=0)
            term = jnp.dot(left, w[k], preferred_element_type=f32)
            new = term if new is None else new + term

        @pl.when(b == 0)
        def _():
            acc[...] = new

        @pl.when(b > 0)
        def _():
            acc[...] += new

        @pl.when(b == bands // 2 - 1)
        def _():
            position = lax.axis_index("band")
            for d in range(count):
                row = pl.multiple_of(jnp.bitwise_xor(position, d) * part, part)
                out[pl.ds(row, part), :] = acc[d * part : (d + 1) * part, :]

    block = pl.BlockSpec((2, part, row_count), lambda b: (b, 0, 0))
    return pl.pallas_call(
        kernel,
        name="summed",
        grid=(bands // 2,),
        in_specs=[
            pl.BlockSpec((2, row_count, wide), lambda b: (b, 0, 0)),
            *([block] * count),
        ],
        out_specs=pl.BlockSpec((count * part, wide), lambda b: (0, 0)),
        out_shape=jax.ShapeDtypeStruct((count * part, wide), f32),
        scratch_shapes=[pltpu.VMEM((count * part, wide), f32)],
        compiler_params=pltpu.CompilerParams(vmem_limit_bytes=60 << 20),
    )(weighted, *pieces)


def swapped(x, axis, size, d):
    return lax.ppermute(x, axis, [(i, i ^ d) for i in range(size)])


def sum_over(x, axis, size):
    if size & (size - 1):
        return lax.psum(x, axis)
    d = 1
    while d < size:
        x = x + swapped(x, axis, size, d)
        d *= 2
    return x


def solution(mesh):
    band_size = mesh.shape["band"]
    pw_size = mesh.shape["pw"]

    def body(strength, frequency, left, right, band_energy, energies, occupied):
        target_count = right.shape[1]
        scalars = (band_energy, energies, occupied)
        direct = band_size in (1, 2, 4, 8) and left.shape[1] % 16 == 0
        if direct:
            pieces = [left] + [swapped(left, "band", band_size, d) for d in range(1, band_size)]
        else:
            left_all = lax.all_gather(left, "band", axis=1, tiled=True)
        weighted = band_call(strength, frequency, right.transpose(0, 2, 1), scalars)
        if direct:
            both = left_call(pieces, weighted)
        else:
            both = jnp.einsum("bng,bgx->nx", left_all, weighted, preferred_element_type=f32)
        parts = both.reshape(band_size, target_count // band_size, -1)
        parts = lax.all_to_all(parts, "band", split_axis=0, concat_axis=0, tiled=True)
        total = sum_over(parts.sum(0), "pw", pw_size)
        even = total[:, :target_count]
        odd = total[:, target_count:] * (0.5 * (energies[1] - energies[0]) / math.sqrt(2.0 * WIDTH))
        return jnp.stack([even - odd, even + odd]) * (1.0 / math.sqrt(2.0 * WIDTH))

    return jax.shard_map(
        body,
        mesh=mesh,
        in_specs=(
            P("pw", "band"),
            P("pw", "band"),
            P(None, "band", "pw"),
            P(None, None, "band"),
            P(),
            P(),
            P(),
        ),
        out_specs=P(None, "band", None),
        check_vma=False,
    )
```

```python
import math

import jax
import jax.numpy as jnp
from jax import lax
from jax.experimental import pallas as pl
from jax.experimental.pallas import tpu as pltpu
from jax.sharding import PartitionSpec as P


WIDTH = 0.01
CHUNK = 256
ROWS = 336
f32, bf16 = jnp.float32, jnp.bfloat16


def rows_of(count):
    return max(r for r in range(16, ROWS + 1, 16) if count % r == 0)


def band_call(strength, frequency, right, scalars):
    row_count, column_count = strength.shape
    bands, _, target_count = right.shape
    rows = rows_of(row_count)
    steps = row_count // rows
    chunks = -(-column_count // CHUNK)
    tail = column_count - (chunks - 1) * CHUNK
    tail_at = column_count - tail
    loops = bands // 2
    unit = 1.0 / math.sqrt(2.0 * WIDTH)

    def kernel(*refs):
        be, en, oc, freq0, str0, freq, stren, right_hbm = refs[:8]
        out, ws, ts, fa, fb, rt, sem = refs[8:]
        g = pl.program_id(0)
        cur = g % 2
        nxt = 1 - cur
        e0 = en[0] * unit
        e1 = en[1] * unit
        half = 0.5 * (e1 - e0)
        k1 = 0.5 - half * half
        k2 = 2.0 * half * half

        def convert(w, s):
            w = w.astype(f32)
            return w * unit, s.astype(f32) / w

        def convert_at(w_ref, s_ref, slot, c):
            lanes = pl.ds(pl.multiple_of(c * CHUNK, CHUNK), CHUNK)
            ws[slot, c], ts[slot, c] = convert(w_ref[:, lanes], s_ref[:, lanes])

        def convert_tail(w_ref, s_ref, slot):
            w, s = convert(w_ref[:, tail_at:column_count], s_ref[:, tail_at:column_count])
            ws[slot, chunks - 1, :, 0:tail] = w
            ts[slot, chunks - 1, :, 0:tail] = s

        def center_of(b):
            sign = (1 - 2 * oc[b]).astype(f32)
            return sign * (0.5 * (e0 + e1) - be[b] * unit)

        def factors(slot, c, lo, center, dst):
            mu = ws[slot, c, pl.ds(lo, 16)] - center
            t = mu * mu + k1
            r = ts[slot, c, pl.ds(lo, 16)] / (t * t + k2)
            x = r * t
            dst[c, pl.ds(lo, 16), :] = (mu * x).astype(bf16)
            dst[c, pl.ds(rows + lo, 16), :] = (r - x).astype(bf16)

        def first_factors(dst):
            center = center_of(0)
            piece = max(p for p in (112, 96, 48, 32, 16) if rows % p == 0)

            def one(c, _):
                def part(k, _):
                    for q in range(0, piece, 16):
                        factors(0, c, pl.multiple_of(k * piece + q, 16), center, dst)
                    return 0

                return lax.fori_loop(0, rows // piece, part, 0)

            lax.fori_loop(0, chunks, one, 0)

        def step(slot, b_next, dst, b, src):
            center = center_of(b_next)
            total = None
            for c in range(chunks):
                for lo in range(0, rows, 16):
                    factors(slot, c, lo, center, dst)
                rhs = rt[b, c * CHUNK : (c + 1) * CHUNK, :]
                part = jnp.dot(src[c], rhs, preferred_element_type=f32)
                total = part if total is None else total + part
            out[b, :, 0:target_count] = total[:rows].astype(bf16)
            out[b, :, target_count:] = total[rows:].astype(bf16)

        def fetch(k):
            part = (pl.ds(0, 2), pl.ds(2, bands - 2))[k]
            return pltpu.make_async_copy(
                right_hbm.at[part], rt.at[part, pl.ds(0, column_count), :], sem.at[k]
            )

        @pl.when(g == 0)
        def _():
            for k in range(2):
                fetch(k).start()
            if column_count < chunks * CHUNK:
                for b in range(bands):
                    rt[b, column_count:, :] = jnp.zeros((chunks * CHUNK - column_count, target_count), bf16)
            for slot in range(2):
                ws[slot, chunks - 1] = jnp.ones((rows, CHUNK), f32)
                ts[slot, chunks - 1] = jnp.zeros((rows, CHUNK), f32)
            convert_tail(freq0, str0, 0)
            if chunks > 1:

                def one(c, _):
                    convert_at(freq0, str0, 0, c)
                    return 0

                lax.fori_loop(0, chunks - 1, one, 0)

            first_factors(fa)
            fetch(0).wait()

        convert_tail(freq, stren, nxt)
        if chunks > 1:

            def ahead_one(c, _):
                convert_at(freq, stren, nxt, c)
                return 0

            lax.fori_loop(0, chunks - 1, ahead_one, 0)

        def pair(i, _):
            @pl.when((g == 0) & (i == 1))
            def _():
                fetch(1).wait()

            step(cur, 2 * i + 1, fb, 2 * i, fa)
            end = i == loops - 1
            step(jnp.where(end, nxt, cur), jnp.where(end, 0, 2 * i + 2), fa, 2 * i + 1, fb)
            return 0

        lax.fori_loop(0, loops, pair, 0)

    smem = pl.BlockSpec(memory_space=pltpu.SMEM)
    start = pl.BlockSpec((rows, column_count), lambda g: (0, 0), pipeline_mode=pl.Buffered(1))
    ahead = pl.BlockSpec((rows, column_count), lambda g: (jnp.minimum(g + 1, steps - 1), 0))
    in_specs = [smem, smem, smem, start, start, ahead, ahead, pl.BlockSpec(memory_space=pl.ANY)]
    operands = [*scalars, frequency, strength, frequency, strength, right]
    scratch = [
        pltpu.VMEM((2, chunks, rows, CHUNK), f32),
        pltpu.VMEM((2, chunks, rows, CHUNK), f32),
        pltpu.VMEM((chunks, 2 * rows, CHUNK), bf16),
        pltpu.VMEM((chunks, 2 * rows, CHUNK), bf16),
        pltpu.VMEM((bands, chunks * CHUNK, target_count), bf16),
        pltpu.SemaphoreType.DMA((2,)),
    ]
    wide = 2 * target_count
    return pl.pallas_call(
        kernel,
        name="weighted",
        grid=(steps,),
        in_specs=in_specs,
        out_specs=pl.BlockSpec((bands, rows, wide), lambda g: (0, g, 0)),
        out_shape=jax.ShapeDtypeStruct((bands, row_count, wide), bf16),
        scratch_shapes=scratch,
        compiler_params=pltpu.CompilerParams(
            vmem_limit_bytes=63 << 20
        ),
    )(*operands)


def left_call(pieces, weighted, occupied):
    bands, part, row_count = pieces[0].shape
    wide = weighted.shape[2]
    count = len(pieces)

    def kernel(*refs):
        oc, w = refs[0], refs[1]
        parts = refs[2 : 2 + count]
        out, acc = refs[2 + count :]
        b = pl.program_id(0)
        new = None
        for k in range(2):
            left = jnp.concatenate([p[k] for p in parts], axis=0)
            term = jnp.dot(left, w[k], preferred_element_type=f32)
            sign = (2 * oc[2 * b + k] - 1).astype(f32)
            term = jnp.concatenate([term[:, : wide // 2] * sign, term[:, wide // 2 :]], axis=1)
            new = term if new is None else new + term

        @pl.when(b == 0)
        def _():
            acc[...] = new

        @pl.when(b > 0)
        def _():
            acc[...] += new

        @pl.when(b == bands // 2 - 1)
        def _():
            position = lax.axis_index("band")
            for d in range(count):
                row = pl.multiple_of(jnp.bitwise_xor(position, d) * part, part)
                out[pl.ds(row, part), :] = acc[d * part : (d + 1) * part, :]

    block = pl.BlockSpec((2, part, row_count), lambda b: (b, 0, 0))
    return pl.pallas_call(
        kernel,
        name="summed",
        grid=(bands // 2,),
        in_specs=[
            pl.BlockSpec(memory_space=pltpu.SMEM),
            pl.BlockSpec((2, row_count, wide), lambda b: (b, 0, 0)),
            *([block] * count),
        ],
        out_specs=pl.BlockSpec((count * part, wide), lambda b: (0, 0)),
        out_shape=jax.ShapeDtypeStruct((count * part, wide), f32),
        scratch_shapes=[pltpu.VMEM((count * part, wide), f32)],
        compiler_params=pltpu.CompilerParams(vmem_limit_bytes=60 << 20),
    )(occupied, weighted, *pieces)


def swapped(x, axis, size, d):
    return lax.ppermute(x, axis, [(i, i ^ d) for i in range(size)])


def sum_over(x, axis, size):
    if size & (size - 1):
        return lax.psum(x, axis)
    d = 1
    while d < size:
        x = x + swapped(x, axis, size, d)
        d *= 2
    return x


def solution(mesh):
    band_size = mesh.shape["band"]
    pw_size = mesh.shape["pw"]

    def body(strength, frequency, left, right, band_energy, energies, occupied):
        target_count = right.shape[1]
        scalars = (band_energy, energies, occupied)
        direct = band_size in (1, 2, 4, 8) and left.shape[1] % 16 == 0
        if direct:
            pieces = [left] + [swapped(left, "band", band_size, d) for d in range(1, band_size)]
        else:
            left_all = lax.all_gather(left, "band", axis=1, tiled=True)
        weighted = band_call(strength, frequency, right.transpose(0, 2, 1), scalars)
        if direct:
            both = left_call(pieces, weighted, occupied)
        else:
            sign = (2 * occupied - 1).astype(bf16)[:, None, None]
            weighted = jnp.concatenate(
                [weighted[..., :target_count] * sign, weighted[..., target_count:]], axis=2
            )
            both = jnp.einsum("bng,bgx->nx", left_all, weighted, preferred_element_type=f32)
        parts = both.reshape(band_size, target_count // band_size, -1)
        parts = lax.all_to_all(parts, "band", split_axis=0, concat_axis=0, tiled=True)
        total = sum_over(parts.sum(0), "pw", pw_size)
        even = total[:, :target_count]
        odd = total[:, target_count:] * (0.5 * (energies[1] - energies[0]) / math.sqrt(2.0 * WIDTH))
        return jnp.stack([even - odd, even + odd]) * (1.0 / math.sqrt(2.0 * WIDTH))

    return jax.shard_map(
        body,
        mesh=mesh,
        in_specs=(
            P("pw", "band"),
            P("pw", "band"),
            P(None, "band", "pw"),
            P(None, None, "band"),
            P(),
            P(),
            P(),
        ),
        out_specs=P(None, "band", None),
        check_vma=False,
    )
```
